32 devices in a mesh: groups: 2 (over y), blk: 4 (over z), win: 4 (over x, core).
Axes of the slice: x: 2, y: 2, z: 4, core: 2. Of those that a mesh axis runs over, the one named last changes fastest.
Arguments:
- spectra: bfloat16 [2, 24, 1024, 201], P(None, 'win', ('groups', 'blk')), parts along dimension 2
- channel_slot: int32 [1024], P(('groups', 'blk')), parts along dimension 0, may hold values from 0 to 511, as said below
- partners: int32 [2, 4], replicated, may hold values from 0 to 3, as said below
Outputs:
- correlations: bfloat16 [2, 1024, 101, 128], P(None, ('groups', 'blk', 'win')), parts along dimension 1
The draws below stay inside these ranges and needn't reach their ends.
There are 2 independent parts, one for each index of `groups`. The reference program is written for one: setup_inputs(seed, part) draws one part's arguments, and reference() takes and returns one part's arrays. A program takes and returns all parts, laid end to end along the dimension named above; an argument that names none is the same for every part. Nothing has to cross between parts.
Inputs may be any that keep to these rules, and one draw needn't show every extreme that they name: channel_slot is a permutation of 0 to 511. For every acquisition shard s (channels s * 128 to s * 128 + 127) and every block b, exactly 32 of the shard's channels go to block b, and they take the slots b * 128 + s * 32 + q for q from 0 to 31. In round r, partners[r, i] = i XOR m_r for one value m_r of 1 to 3 per round; the rounds' values differ.
All inputs are finite; a program needn't handle non-finite values.
Results may differ from the reference program's by a relative error of at most 0.0057.
Values may be sent and summed in bfloat16 or wider, within the bound.
A program may use at most 128 MiB of HBM per device.

```python
import math
import jax
import jax.numpy as jnp
from jax import lax

CH = 128
F = 201
L = 101
ROUNDS = 2
NB = 4
CHANNEL_COUNT = 512
WINDOW_COUNT = 24


def draw_spectra(key, part):
    noise_key = jax.random.fold_in(key, 11)
    transient_event_key = jax.random.fold_in(key, 12)
    colour_key = jax.random.fold_in(key, 13)
    gain_key = jax.random.fold_in(key, 15)
    linear_trend = 3.0 ** (jnp.arange(WINDOW_COUNT, dtype=jnp.float32) / (WINDOW_COUNT - 1))
    transient_event = jnp.exp(jax.random.uniform(transient_event_key, (WINDOW_COUNT, CHANNEL_COUNT), jnp.float32, -math.log(2.0), math.log(2.0)))
    spectral_tint = jnp.exp(jax.random.uniform(colour_key, (CHANNEL_COUNT, F), jnp.float32, math.log(0.3), math.log(3.0)))
    channel_gain = jnp.exp(jax.random.uniform(gain_key, (CHANNEL_COUNT,), jnp.float32, 0.0, math.log(10.0)))
    background_noise = jax.random.normal(noise_key, (2, WINDOW_COUNT, CHANNEL_COUNT, F), jnp.float32)
    value_array = background_noise * linear_trend[None, :, None, None] * transient_event[None, :, :, None] * spectral_tint[None, None, :, :]
    value_array = value_array * channel_gain[None, None, :, None]
    return value_array.astype(jnp.bfloat16)


def draw_channel_slot(key, part):
    per_peer = CH // NB
    keys = jax.random.split(jax.random.fold_in(key, 21), NB)
    orders = jax.vmap(lambda k: jax.random.permutation(k, CH))(keys).astype(jnp.int32)
    shard = jnp.arange(NB, dtype=jnp.int32)[:, None]
    block = orders % NB
    place = orders // NB
    slot = block * CH + shard * per_peer + place
    return slot.reshape(NB * CH).astype(jnp.int32)


def draw_partners(key, part):
    masks = jax.random.permutation(jax.random.fold_in(key, 31), NB - 1)[:ROUNDS].astype(jnp.int32) + 1
    index = jnp.arange(NB, dtype=jnp.int32)
    return jnp.bitwise_xor(index[None, :], masks[:, None]).astype(jnp.int32)


def setup_inputs(seed: int = 0, part: int = 0) -> dict:
    key_of = jax.random.split(jax.random.key(seed), 4)
    part_keys = jax.random.split(jax.random.fold_in(key_of[3], part), 4)
    return {
        "spectra": draw_spectra(jax.random.fold_in(jax.random.fold_in(key_of[3], part), 71), part),
        "channel_slot": draw_channel_slot(jax.random.fold_in(jax.random.fold_in(key_of[3], part), 71), part),
        "partners": draw_partners(jax.random.fold_in(key_of[3], 71), part),
    }


eps_power = 1e-06
half_band = 2

def band_mean(power, windows):
    nbins = power.shape[1]
    padded = jnp.pad(power, ((0, 0), (half_band, half_band)))
    ones = jnp.pad(jnp.ones((nbins,), jnp.float32), (half_band, half_band))
    total = padded[:, 0:nbins]
    count = ones[0:nbins]
    for offset in range(1, 2 * half_band + 1):
        total = total + padded[:, offset:offset + nbins]
        count = count + ones[offset:offset + nbins]
    return total / (count * windows)

def whiten(parts, power, windows):
    scale = lax.rsqrt(band_mean(power, windows) + eps_power)
    return (parts.astype(jnp.float32) * scale).astype(jnp.bfloat16)

def lag_table(nbins, nlags, windows):
    samples = 2 * (nbins - 1)
    freq = jnp.arange(nbins, dtype=jnp.int32)
    lags = jnp.arange(nlags, dtype=jnp.int32) - (nlags - 1) // 2
    phase_index = freq[:, None] * lags[None, :] % samples
    angle = 2.0 * math.pi / samples * phase_index.astype(jnp.float32)
    weight = jnp.where((freq == 0) | (freq == nbins - 1), 1.0, 2.0).astype(jnp.float32)
    norm = 1.0 / math.sqrt(windows * samples)
    cos_part = weight[:, None] * jnp.cos(angle) * norm
    sin_part = -weight[:, None] * jnp.sin(angle) * norm
    return jnp.concatenate([cos_part, sin_part], axis=0)

def correlate(sources, receivers, table):
    left = jnp.concatenate([sources[0], sources[1]], axis=0).astype(jnp.float32)
    turned = jnp.concatenate([sources[1], -sources[0]], axis=0).astype(jnp.float32)
    right = jnp.concatenate([receivers[0], receivers[1]], axis=0).astype(jnp.float32)
    tile = 32
    count = left.shape[1] // tile

    def one_tile(index):
        start = index * tile
        part_left = lax.dynamic_slice_in_dim(left, start, tile, 1)
        part_turned = lax.dynamic_slice_in_dim(turned, start, tile, 1)
        real = jnp.einsum('wak,wbk->kab', part_left, right, precision=lax.Precision.HIGHEST)
        imag = jnp.einsum('wak,wbk->kab', part_turned, right, precision=lax.Precision.HIGHEST)
        stacked = jnp.concatenate([real, imag], axis=0)
        return jnp.einsum('kab,kl->alb', stacked, table, precision=lax.Precision.HIGHEST)
    result = lax.map(one_tile, jnp.arange(count, dtype=jnp.int32))
    return result.reshape(count * tile, table.shape[1], right.shape[1]).astype(jnp.bfloat16)

def reference(spectra, channel_slot, partners):
    blocked = jnp.zeros_like(spectra).at[:, :, channel_slot, :].set(spectra)
    value_array = blocked.astype(jnp.float32)
    power = lax.optimization_barrier(jnp.sum(value_array * value_array, axis=(0, 1)))
    white = whiten(blocked, power, WINDOW_COUNT)
    grouped = white.reshape(2, WINDOW_COUNT, NB, CH, F)
    table = lag_table(F, L, WINDOW_COUNT)
    rounds = []
    for round_index in range(ROUNDS):

        def per_block(index):
            own = lax.dynamic_index_in_dim(grouped, index, 2, keepdims=False)
            other = lax.dynamic_index_in_dim(grouped, partners[round_index, index].astype(jnp.int32), 2, keepdims=False)
            return correlate(own, other, table)
        result = lax.map(per_block, jnp.arange(NB, dtype=jnp.int32))
        rounds.append(result.reshape(NB * CH, L, CH))
    return jnp.stack(rounds, axis=0)
```

```python
import math

import jax
import jax.numpy as jnp
from jax import lax
from jax.sharding import PartitionSpec as P

L = 101
ROUNDS = 2


eps_power = 1e-06
half_band = 2
tile_rows = 8


def shortened(value):

    def short(part):
        return part.astype(jnp.bfloat16) if part.dtype == jnp.float32 else part

    return jax.tree.map(short, value)


def partner(value, axis, distance):
    mask = 2**distance
    pairs = [(source, source ^ mask) for source in range(lax.axis_size(axis))]
    return lax.ppermute(value, axis, pairs)


def band_mean(power, windows):
    nbins = power.shape[1]
    padded = jnp.pad(power, ((0, 0), (half_band, half_band)))
    ones = jnp.pad(jnp.ones((nbins,), jnp.float32), (half_band, half_band))
    total = padded[:, 0:nbins]
    count = ones[0:nbins]
    for offset in range(1, 2 * half_band + 1):
        total = total + padded[:, offset : offset + nbins]
        count = count + ones[offset : offset + nbins]
    return total / (count * windows)


def power_of(parts):
    value_array = parts.astype(jnp.float32)
    return jnp.sum(value_array * value_array, axis=(0, 1))


def whiten(parts, power, windows):
    scale = lax.rsqrt(band_mean(power, windows) + eps_power)
    return (parts.astype(jnp.float32) * scale).astype(jnp.bfloat16)


def lag_table(nbins, nlags, windows):
    samples = 2 * (nbins - 1)
    freq = jnp.arange(nbins, dtype=jnp.int32)
    lags = jnp.arange(nlags, dtype=jnp.int32) - (nlags - 1) // 2
    phase_index = freq[:, None] * lags[None, :] % samples
    angle = 2.0 * math.pi / samples * phase_index.astype(jnp.float32)
    weight = jnp.where((freq == 0) | (freq == nbins - 1), 1.0, 2.0).astype(jnp.float32)
    norm = 1.0 / math.sqrt(windows * samples)
    cos_part = weight[:, None] * jnp.cos(angle) * norm
    sin_part = -weight[:, None] * jnp.sin(angle) * norm
    return jnp.concatenate([cos_part, sin_part], axis=0)


def correlate(sources, receivers, table):
    left = jnp.concatenate([sources[0], sources[1]], axis=0)
    turned = jnp.concatenate([sources[1], -sources[0]], axis=0)
    right = jnp.concatenate([receivers[0], receivers[1]], axis=0)
    both = jnp.stack([left, turned], axis=1)
    cross = jnp.einsum(
        "wcak,wbk->kcab", both, right, preferred_element_type=jnp.float32
    ).astype(jnp.bfloat16)
    return jnp.einsum(
        "kcab,ckl->alb", cross, table, preferred_element_type=jnp.float32
    ).astype(jnp.bfloat16)


def whiten_all(parts):
    return whiten(parts, power_of(parts), parts.shape[1])


def body(spectra, channel_slot, partners):
    n_blk = lax.axis_size("blk")
    n_win = lax.axis_size("win")
    chans = spectra.shape[2]
    nbins = spectra.shape[3]
    per_peer = chans // n_blk
    here = lax.axis_index("blk")
    target = channel_slot // chans * per_peer + channel_slot % chans - here * per_peer
    selector = (jnp.arange(chans, dtype=jnp.int32)[:, None] == target[None, :]).astype(jnp.bfloat16)
    ordered = jnp.einsum(
        "pc,rwcf->rwpf", selector, spectra, preferred_element_type=jnp.float32
    ).astype(jnp.bfloat16)
    blocked = lax.all_to_all(ordered, "blk", split_axis=2, concat_axis=2, tiled=True)
    windows = spectra.shape[1] * n_win
    share = chans // n_win
    own_all = lax.all_gather(blocked, "win", axis=1, tiled=True)
    sources = lax.dynamic_slice_in_dim(own_all, lax.axis_index("win") * share, share, 2)
    sources = whiten_all(sources)
    table = lag_table(nbins, L, windows).reshape(2, nbins, L).astype(jnp.bfloat16)
    masks = jnp.bitwise_xor(partners[:, here], here)

    def mover(mask):
        pairs = [(source, source ^ mask) for source in range(n_blk)]
        return lambda value: lax.ppermute(value, "blk", pairs)

    movers = [mover(mask) for mask in range(1, n_blk)]
    results = []
    for round_index in range(ROUNDS):
        moving = lax.switch(masks[round_index] - 1, movers, blocked)
        partner_all = lax.all_gather(moving, "win", axis=1, tiled=True)
        results.append(correlate(sources, whiten_all(partner_all), table))
    return jnp.stack(results, axis=0)


def solution(mesh):
    in_specs = (P(None, "win", ("groups", "blk"), None), P(("groups", "blk")), P())
    out_specs = P(None, ("groups", "blk", "win"), None, None)
    return jax.shard_map(body, mesh=mesh, in_specs=in_specs, out_specs=out_specs, check_vma=False)
```

```python
import functools
import math

import jax
import jax.numpy as jnp
from jax import lax
from jax.experimental import pallas as pl
from jax.experimental.pallas import tpu as pltpu
from jax.sharding import PartitionSpec as P

L = 101
ROUNDS = 2


eps_power = 1e-06
half_band = 2
tile_rows = 8


def band_mean(power, windows):
    nbins = power.shape[1]
    padded = jnp.pad(power, ((0, 0), (half_band, half_band)))
    ones = jnp.pad(jnp.ones((nbins,), jnp.float32), (half_band, half_band))
    total = padded[:, 0:nbins]
    count = ones[0:nbins]
    for offset in range(1, 2 * half_band + 1):
        total = total + padded[:, offset : offset + nbins]
        count = count + ones[offset : offset + nbins]
    return total / (count * windows)


def whiten(parts, power, windows):
    scale = lax.rsqrt(band_mean(power, windows) + eps_power)
    return (parts.astype(jnp.float32) * scale).astype(jnp.bfloat16)


def lag_table(nbins, nlags, windows):
    samples = 2 * (nbins - 1)
    freq = jnp.arange(nbins, dtype=jnp.int32)
    lags = jnp.arange(nlags, dtype=jnp.int32) - (nlags - 1) // 2
    phase_index = freq[:, None] * lags[None, :] % samples
    angle = 2.0 * math.pi / samples * phase_index.astype(jnp.float32)
    weight = jnp.where((freq == 0) | (freq == nbins - 1), 1.0, 2.0).astype(jnp.float32)
    norm = 1.0 / math.sqrt(windows * samples)
    cos_part = weight[:, None] * jnp.cos(angle) * norm
    sin_part = -weight[:, None] * jnp.sin(angle) * norm
    return jnp.concatenate([cos_part, sin_part], axis=0)


def correlate(both, right, table):
    cross = jnp.einsum(
        "wcak,wbk->kcab", both, right, preferred_element_type=jnp.float32
    ).astype(jnp.bfloat16)
    return jnp.einsum(
        "kcab,ckl->alb", cross, table, preferred_element_type=jnp.float32
    ).astype(jnp.bfloat16)


def whiten_all(parts, windows):
    value_array = parts.astype(jnp.float32)
    power = jnp.sum(value_array * value_array, axis=0)
    return whiten(parts, power, windows)


def flip(index, bit):
    return index + bit - 2 * bit * ((index // bit) % 2)


def exchange_kernel(
    n_blk, n_win, pair_ref, own_ref, got_ref, src_ref, pair_stage, own_stage,
    pair_send, pair_recv, pass_send, pass_recv, own_send, own_recv, local_sem
):
    blk = lax.axis_index("blk")
    win = lax.axis_index("win")
    per_share = n_blk // n_win
    barrier = pltpu.get_barrier_semaphore()
    for step in range(1, n_blk * n_win):
        other = (blk * n_win + win + step) % (n_blk * n_win)
        pl.semaphore_signal(
            barrier,
            inc=1,
            device_id={"blk": other // n_win, "win": other % n_win},
            device_id_type=pl.DeviceIdType.MESH,
        )
    pl.semaphore_wait(barrier, n_blk * n_win - 1)

    def remote(src, dst, send, recv, to_blk, to_win):
        return pltpu.make_async_remote_copy(
            src_ref=src,
            dst_ref=dst,
            send_sem=send,
            recv_sem=recv,
            device_id={"blk": to_blk, "win": to_win},
            device_id_type=pl.DeviceIdType.MESH,
        )

    bits = []
    bit = n_win // 2
    while bit:
        bits.append(bit)
        bit //= 2

    def direct(step):
        dest = (blk + step) % n_blk
        return remote(
            pair_ref.at[:, :, dest], got_ref.at[:, win, :, blk],
            pair_send.at[step], pair_recv.at[step], dest, win,
        )

    user = blk // per_share
    place = blk % per_share

    def own(step):
        dest = (blk + step) % n_blk
        return remote(
            own_ref.at[:, dest], src_ref.at[win, :, place],
            own_send.at[step], own_recv.at[place * n_win + win], dest, user,
        )

    def passed(step, offset, over):
        origin = (blk + n_blk - step) % n_blk
        slot = win
        for each in bits:
            if offset & each:
                slot = flip(slot, each)
        target = got_ref.at[:, slot, :, origin]
        source = pair_ref.at[:, :, blk] if step == 0 and offset == 0 else target
        mark = (offset | over) - 1
        return remote(
            source, target, pass_send.at[mark, step], pass_recv.at[mark, step], blk, flip(win, over)
        )

    stage_in = pltpu.make_async_copy(pair_ref.at[:, :, blk], pair_stage, local_sem.at[0])
    stage_in.start()
    is_user = user == win

    def own_in():
        return pltpu.make_async_copy(own_ref.at[:, blk], own_stage, local_sem.at[1])

    def own_out():
        return pltpu.make_async_copy(own_stage, src_ref.at[win, :, place], local_sem.at[2])

    @pl.when(is_user)
    def _():
        own_in().start()

    passes = []
    held = [0]
    for over in bits:
        passes.extend((offset, over) for offset in held)
        held = held + [offset | over for offset in held]

    sends = []
    for offset, over in passes:
        if offset == 0:
            copy = passed(0, 0, over)
            copy.start()
            sends.append(copy)
    for step in range(1, n_blk):
        copy = direct(step)
        copy.start()
        sends.append(copy)
    for step in range(1, n_blk):
        copy = own(step)
        copy.start()
        sends.append(copy)

    @pl.when(jnp.logical_not(is_user))
    def _():
        own(0).start()

    stage_in.wait()
    stage_out = pltpu.make_async_copy(pair_stage, got_ref.at[:, win, :, blk], local_sem.at[3])
    stage_out.start()

    @pl.when(is_user)
    def _():
        own_in().wait()
        own_out().start()

    waited = set()

    def arrive(step, offset):
        if (step, offset) in waited:
            return
        waited.add((step, offset))
        if offset == 0:
            if step:
                direct(step).wait_recv()
        else:
            over = offset & -offset
            passed(step, offset - over, over).wait_recv()

    for step in range(n_blk + 1):
        if 1 <= step < n_blk:
            arrive(step, 0)
            for offset, over in passes:
                if offset == 0:
                    copy = passed(step, 0, over)
                    copy.start()
                    sends.append(copy)
        if step >= 1:
            for offset, over in passes:
                if offset:
                    arrive(step - 1, offset)
                    copy = passed(step - 1, offset, over)
                    copy.start()
                    sends.append(copy)
    for step in range(n_blk):
        for offset in held:
            arrive(step, offset)

    for local in range(per_share):
        for peer in range(n_win):
            here = jnp.logical_and(blk == win * per_share + local, win == peer)

            @pl.when(jnp.logical_not(here))
            def _():
                piece = src_ref.at[peer, :, local]
                remote(
                    piece, piece, own_send.at[0], own_recv.at[local * n_win + peer], blk, win
                ).wait_recv()

    for copy in sends:
        copy.wait_send()

    @pl.when(jnp.logical_not(is_user))
    def _():
        own(0).wait_send()

    stage_out.wait()

    @pl.when(is_user)
    def _():
        own_out().wait()


def exchange(pair, own, n_blk, n_win):
    rounds, rows, _, per_peer, nbins = pair.shape
    per_share = n_blk // n_win
    dtype = pair.dtype
    anywhere = pl.BlockSpec(memory_space=pl.ANY)
    return pl.pallas_call(
        functools.partial(exchange_kernel, n_blk, n_win),
        out_shape=(
            jax.ShapeDtypeStruct((rounds, n_win, rows, n_blk, per_peer, nbins), dtype),
            jax.ShapeDtypeStruct((n_win, rows, per_share, per_peer, nbins), dtype),
        ),
        in_specs=[anywhere, anywhere],
        out_specs=(anywhere, anywhere),
        scratch_shapes=[
            pltpu.VMEM((rounds, rows, per_peer, nbins), dtype),
            pltpu.VMEM((rows, per_peer, nbins), dtype),
            pltpu.SemaphoreType.DMA((n_blk,)),
            pltpu.SemaphoreType.DMA((n_blk,)),
            pltpu.SemaphoreType.DMA((n_win - 1, n_blk)),
            pltpu.SemaphoreType.DMA((n_win - 1, n_blk)),
            pltpu.SemaphoreType.DMA((n_blk,)),
            pltpu.SemaphoreType.DMA((n_blk,)),
            pltpu.SemaphoreType.DMA((4,)),
        ],
        compiler_params=pltpu.CompilerParams(collective_id=0, has_side_effects=True),
    )(pair, own)


def body(spectra, channel_slot, partners):
    n_blk = lax.axis_size("blk")
    n_win = lax.axis_size("win")
    parts, mine, chans, nbins = spectra.shape
    rows = parts * mine
    per_peer = chans // n_blk
    here = lax.axis_index("blk")
    share = chans // n_win
    windows = mine * n_win
    flat = spectra.reshape(rows, chans, nbins)
    wanted = jnp.concatenate([partners, jnp.arange(n_blk, dtype=jnp.int32)[None]], axis=0)
    slots = (
        wanted[:, :, None] * chans
        + here * per_peer
        + jnp.arange(per_peer, dtype=jnp.int32)[None, None, :]
    )
    selector = (slots[..., None] == channel_slot).astype(jnp.bfloat16)
    pair = jnp.einsum(
        "tzqc,xcf->txzqf", selector[:ROUNDS], flat, preferred_element_type=jnp.float32
    ).astype(jnp.bfloat16)
    own = jnp.einsum(
        "zqc,xcf->xzqf", selector[ROUNDS], flat, preferred_element_type=jnp.float32
    ).astype(jnp.bfloat16)
    got, mine_all = exchange(pair, own, n_blk, n_win)
    sources = whiten_all(mine_all.reshape(n_win * rows, share, nbins), windows)
    split = sources.reshape(n_win, parts, mine, share, nbins)
    turned = jnp.stack([split[:, 1], -split[:, 0]], axis=1).reshape(sources.shape)
    both = jnp.stack([sources, turned], axis=1)
    table = lag_table(nbins, L, windows).reshape(2, nbins, L).astype(jnp.bfloat16)
    results = []
    for round_index in range(ROUNDS):
        right = got[round_index].reshape(n_win * rows, chans, nbins)
        results.append(correlate(both, whiten_all(right, windows), table))
    return jnp.stack(results, axis=0)


def solution(mesh):
    in_specs = (P(None, "win", ("groups", "blk"), None), P(("groups", "blk")), P())
    out_specs = P(None, ("groups", "blk", "win"), None, None)
    return jax.shard_map(body, mesh=mesh, in_specs=in_specs, out_specs=out_specs, check_vma=False)
```

```python
import functools
import math

import jax
import jax.numpy as jnp
from jax import lax
from jax.experimental import pallas as pl
from jax.experimental.pallas import tpu as pltpu
from jax.sharding import PartitionSpec as P

L = 101
ROUNDS = 2


eps_power = 1e-06
half_band = 2
tile_rows = 8


def whiten_kernel(values_ref, out_ref):
    n_win, rows, _, _, nbins = values_ref.shape[1:]
    half = rows // 2
    power = None
    for win in range(n_win):
        value_array = values_ref[0, win, :, 0].astype(jnp.float32)
        part = jnp.sum(value_array * value_array, axis=0)
        power = part if power is None else power + part
    padding = jnp.zeros((power.shape[0], half_band), jnp.float32)
    padded = jnp.concatenate([padding, power, padding], axis=1)
    total = padded[:, 0:nbins]
    for offset in range(1, 2 * half_band + 1):
        total = total + padded[:, offset : offset + nbins]
    place = lax.broadcasted_iota(jnp.int32, power.shape, 1)
    count = 1 + jnp.minimum(place, half_band) + jnp.minimum(nbins - 1 - place, half_band)
    windows = n_win * rows // 2
    level = total / (count.astype(jnp.float32) * windows)
    scale = lax.rsqrt(level + eps_power)
    for win in range(n_win):
        value_array = values_ref[0, win, :, 0].astype(jnp.float32)
        white = (value_array * scale).astype(out_ref.dtype)
        out_ref[0, pl.ds(win * rows, rows), 0] = white
        if out_ref.shape[0] == 2:
            out_ref[1, pl.ds(win * rows, half), 0] = white[half:]
            out_ref[1, pl.ds(win * rows + half, half), 0] = -white[:half]


def whiten_all(values, index, forms):
    _, n_win, rows, shards, per_peer, nbins = values.shape
    out = pl.pallas_call(
        whiten_kernel,
        grid=(shards,),
        out_shape=jax.ShapeDtypeStruct((forms, n_win * rows, shards, per_peer, nbins), values.dtype),
        in_specs=[
            pl.BlockSpec((1, n_win, rows, 1, per_peer, nbins), lambda s: (index, 0, 0, s, 0, 0))
        ],
        out_specs=pl.BlockSpec((forms, n_win * rows, 1, per_peer, nbins), lambda s: (0, 0, s, 0, 0)),
    )(values)
    return out.reshape(forms, n_win * rows, shards * per_peer, nbins)


def lag_table(nbins, nlags, windows):
    samples = 2 * (nbins - 1)
    freq = jnp.arange(nbins, dtype=jnp.int32)
    lags = jnp.arange(nlags, dtype=jnp.int32) - (nlags - 1) // 2
    phase_index = freq[:, None] * lags[None, :] % samples
    angle = 2.0 * math.pi / samples * phase_index.astype(jnp.float32)
    weight = jnp.where((freq == 0) | (freq == nbins - 1), 1.0, 2.0).astype(jnp.float32)
    norm = 1.0 / math.sqrt(windows * samples)
    cos_part = weight[:, None] * jnp.cos(angle) * norm
    sin_part = -weight[:, None] * jnp.sin(angle) * norm
    return jnp.concatenate([cos_part, sin_part], axis=0)


def correlate(both, right, table):
    cross = jnp.einsum(
        "cwak,wbk->kcab", both, right, preferred_element_type=jnp.float32
    ).astype(jnp.bfloat16)
    return jnp.einsum(
        "kcab,ckl->lab", cross, table, preferred_element_type=jnp.float32
    ).astype(jnp.bfloat16)


def flip(index, bit):
    return index + bit - 2 * bit * ((index // bit) % 2)


def exchange_kernel(
    n_blk, n_win, pair_ref, own_ref, got_ref, src_ref, pair_stage, own_stage,
    pair_send, pair_recv, pass_send, pass_recv, own_send, own_recv, local_sem
):
    blk = lax.axis_index("blk")
    win = lax.axis_index("win")
    per_share = n_blk // n_win
    barrier = pltpu.get_barrier_semaphore()
    for step in range(1, n_blk * n_win):
        other = (blk * n_win + win + step) % (n_blk * n_win)
        pl.semaphore_signal(
            barrier,
            inc=1,
            device_id={"blk": other // n_win, "win": other % n_win},
            device_id_type=pl.DeviceIdType.MESH,
        )
    pl.semaphore_wait(barrier, n_blk * n_win - 1)

    def remote(src, dst, send, recv, to_blk, to_win):
        return pltpu.make_async_remote_copy(
            src_ref=src,
            dst_ref=dst,
            send_sem=send,
            recv_sem=recv,
            device_id={"blk": to_blk, "win": to_win},
            device_id_type=pl.DeviceIdType.MESH,
        )

    bits = []
    bit = n_win // 2
    while bit:
        bits.append(bit)
        bit //= 2

    def direct(step):
        dest = (blk + step) % n_blk
        return remote(
            pair_ref.at[:, :, dest], got_ref.at[:, win, :, blk],
            pair_send.at[step], pair_recv.at[step], dest, win,
        )

    user = blk // per_share
    place = blk % per_share

    def own(step):
        dest = (blk + step) % n_blk
        return remote(
            own_ref.at[:, dest], src_ref.at[win, :, place],
            own_send.at[step], own_recv.at[place * n_win + win], dest, user,
        )

    def passed(step, offset, over):
        origin = (blk + n_blk - step) % n_blk
        slot = win
        for each in bits:
            if offset & each:
                slot = flip(slot, each)
        target = got_ref.at[:, slot, :, origin]
        source = pair_ref.at[:, :, blk] if step == 0 and offset == 0 else target
        mark = (offset | over) - 1
        return remote(
            source, target, pass_send.at[mark, step], pass_recv.at[mark, step], blk, flip(win, over)
        )

    stage_in = pltpu.make_async_copy(pair_ref.at[:, :, blk], pair_stage, local_sem.at[0])
    stage_in.start()
    is_user = user == win

    def own_in():
        return pltpu.make_async_copy(own_ref.at[:, blk], own_stage, local_sem.at[1])

    def own_out():
        return pltpu.make_async_copy(own_stage, src_ref.at[win, :, place], local_sem.at[2])

    @pl.when(is_user)
    def _():
        own_in().start()

    passes = []
    held = [0]
    for over in bits:
        passes.extend((offset, over) for offset in held)
        held = held + [offset | over for offset in held]

    sends = []
    for offset, over in passes:
        if offset == 0:
            copy = passed(0, 0, over)
            copy.start()
            sends.append(copy)
    for step in range(1, n_blk):
        copy = direct(step)
        copy.start()
        sends.append(copy)
    for step in range(1, n_blk):
        copy = own(step)
        copy.start()
        sends.append(copy)

    @pl.when(jnp.logical_not(is_user))
    def _():
        own(0).start()

    stage_in.wait()
    stage_out = pltpu.make_async_copy(pair_stage, got_ref.at[:, win, :, blk], local_sem.at[3])
    stage_out.start()

    @pl.when(is_user)
    def _():
        own_in().wait()
        own_out().start()

    waited = set()

    def arrive(step, offset):
        if (step, offset) in waited:
            return
        waited.add((step, offset))
        if offset == 0:
            if step:
                direct(step).wait_recv()
        else:
            over = offset & -offset
            passed(step, offset - over, over).wait_recv()

    for step in range(n_blk + 1):
        if 1 <= step < n_blk:
            arrive(step, 0)
            for offset, over in passes:
                if offset == 0:
                    copy = passed(step, 0, over)
                    copy.start()
                    sends.append(copy)
        if step >= 1:
            for offset, over in passes:
                if offset:
                    arrive(step - 1, offset)
                    copy = passed(step - 1, offset, over)
                    copy.start()
                    sends.append(copy)
    for step in range(n_blk):
        for offset in held:
            arrive(step, offset)

    for local in range(per_share):
        for peer in range(n_win):
            here = jnp.logical_and(blk == win * per_share + local, win == peer)

            @pl.when(jnp.logical_not(here))
            def _():
                piece = src_ref.at[peer, :, local]
                remote(
                    piece, piece, own_send.at[0], own_recv.at[local * n_win + peer], blk, win
                ).wait_recv()

    for copy in sends:
        copy.wait_send()

    @pl.when(jnp.logical_not(is_user))
    def _():
        own(0).wait_send()

    stage_out.wait()

    @pl.when(is_user)
    def _():
        own_out().wait()


def exchange(pair, own, n_blk, n_win):
    rounds, rows, _, per_peer, nbins = pair.shape
    per_share = n_blk // n_win
    dtype = pair.dtype
    anywhere = pl.BlockSpec(memory_space=pl.ANY)
    return pl.pallas_call(
        functools.partial(exchange_kernel, n_blk, n_win),
        out_shape=(
            jax.ShapeDtypeStruct((rounds, n_win, rows, n_blk, per_peer, nbins), dtype),
            jax.ShapeDtypeStruct((n_win, rows, per_share, per_peer, nbins), dtype),
        ),
        in_specs=[anywhere, anywhere],
        out_specs=(anywhere, anywhere),
        scratch_shapes=[
            pltpu.VMEM((rounds, rows, per_peer, nbins), dtype),
            pltpu.VMEM((rows, per_peer, nbins), dtype),
            pltpu.SemaphoreType.DMA((n_blk,)),
            pltpu.SemaphoreType.DMA((n_blk,)),
            pltpu.SemaphoreType.DMA((n_win - 1, n_blk)),
            pltpu.SemaphoreType.DMA((n_win - 1, n_blk)),
            pltpu.SemaphoreType.DMA((n_blk,)),
            pltpu.SemaphoreType.DMA((n_blk,)),
            pltpu.SemaphoreType.DMA((4,)),
        ],
        compiler_params=pltpu.CompilerParams(collective_id=0, has_side_effects=True),
    )(pair, own)


def body(spectra, channel_slot, partners):
    n_blk = lax.axis_size("blk")
    n_win = lax.axis_size("win")
    parts, mine, chans, nbins = spectra.shape
    rows = parts * mine
    per_peer = chans // n_blk
    here = lax.axis_index("blk")
    share = chans // n_win
    windows = mine * n_win
    flat = spectra.reshape(rows, chans, nbins)
    wanted = jnp.concatenate([partners, jnp.arange(n_blk, dtype=jnp.int32)[None]], axis=0)
    slots = (
        wanted[:, :, None] * chans
        + here * per_peer
        + jnp.arange(per_peer, dtype=jnp.int32)[None, None, :]
    )
    selector = (slots[..., None] == channel_slot).astype(jnp.bfloat16)
    pair = jnp.einsum(
        "tzqc,xcf->txzqf", selector[:ROUNDS], flat, preferred_element_type=jnp.float32
    ).astype(jnp.bfloat16)
    own = jnp.einsum(
        "zqc,xcf->xzqf", selector[ROUNDS], flat, preferred_element_type=jnp.float32
    ).astype(jnp.bfloat16)
    got, mine_all = exchange(pair, own, n_blk, n_win)
    both = whiten_all(mine_all[None], 0, 2)
    table = lag_table(nbins, L, windows).reshape(2, nbins, L).astype(jnp.bfloat16)
    results = [
        correlate(both, whiten_all(got, index, 1)[0], table) for index in range(ROUNDS)
    ]
    return jnp.stack(results, axis=0).transpose(0, 2, 1, 3)


def solution(mesh):
    in_specs = (P(None, "win", ("groups", "blk"), None), P(("groups", "blk")), P())
    out_specs = P(None, ("groups", "blk", "win"), None, None)
    return jax.shard_map(body, mesh=mesh, in_specs=in_specs, out_specs=out_specs, check_vma=False)
```

```python
import functools
import math

import jax
import jax.numpy as jnp
from jax import lax
from jax.experimental import pallas as pl
from jax.experimental.pallas import tpu as pltpu
from jax.sharding import PartitionSpec as P

L = 101
ROUNDS = 2


eps_power = 1e-06
half_band = 2
tile_rows = 8


def whiten_into(piece, store, n_win, rows):
    power = None
    for win in range(n_win):
        value_array = piece(win).astype(jnp.float32)
        part = jnp.sum(value_array * value_array, axis=0)
        power = part if power is None else power + part
    nbins = power.shape[1]
    padding = jnp.zeros((power.shape[0], half_band), jnp.float32)
    padded = jnp.concatenate([padding, power, padding], axis=1)
    total = padded[:, 0:nbins]
    for offset in range(1, 2 * half_band + 1):
        total = total + padded[:, offset : offset + nbins]
    place = lax.broadcasted_iota(jnp.int32, power.shape, 1)
    count = 1 + jnp.minimum(place, half_band) + jnp.minimum(nbins - 1 - place, half_band)
    level = total / (count.astype(jnp.float32) * (n_win * rows // 2))
    scale = lax.rsqrt(level + eps_power)
    for win in range(n_win):
        store(win, (piece(win).astype(jnp.float32) * scale).astype(jnp.bfloat16))


def lag_table(nbins, nlags, windows):
    samples = 2 * (nbins - 1)
    freq = jnp.arange(nbins, dtype=jnp.int32)
    lags = jnp.arange(nlags, dtype=jnp.int32) - (nlags - 1) // 2
    phase_index = freq[:, None] * lags[None, :] % samples
    angle = 2.0 * math.pi / samples * phase_index.astype(jnp.float32)
    weight = jnp.where((freq == 0) | (freq == nbins - 1), 1.0, 2.0).astype(jnp.float32)
    norm = 1.0 / math.sqrt(windows * samples)
    cos_part = weight[:, None] * jnp.cos(angle) * norm
    sin_part = -weight[:, None] * jnp.sin(angle) * norm
    return jnp.concatenate([cos_part, sin_part], axis=0)


def correlate(both, right, table):
    cross = jnp.einsum(
        "cwak,wbk->kcab", both, right, preferred_element_type=jnp.float32
    ).astype(jnp.bfloat16)
    return jnp.einsum(
        "kcab,ckl->lab", cross, table, preferred_element_type=jnp.float32
    ).astype(jnp.bfloat16)


def flip(index, bit):
    return index + bit - 2 * bit * ((index // bit) % 2)


def exchange_kernel(
    n_blk, n_win, rounds, pair_ref, own_ref, *refs
):
    right_refs = refs[:rounds]
    both_ref, got_ref, src_ref, pair_send, pair_recv = refs[rounds : rounds + 5]
    pass_send, pass_recv, own_send, own_recv, local_sem = refs[rounds + 5 :]
    blk = lax.axis_index("blk")
    win = lax.axis_index("win")
    per_share = n_blk // n_win
    barrier = pltpu.get_barrier_semaphore()
    for step in range(1, n_blk * n_win):
        other = (blk * n_win + win + step) % (n_blk * n_win)
        pl.semaphore_signal(
            barrier,
            inc=1,
            device_id={"blk": other // n_win, "win": other % n_win},
            device_id_type=pl.DeviceIdType.MESH,
        )
    pl.semaphore_wait(barrier, n_blk * n_win - 1)

    def remote(src, dst, send, recv, to_blk, to_win):
        return pltpu.make_async_remote_copy(
            src_ref=src,
            dst_ref=dst,
            send_sem=send,
            recv_sem=recv,
            device_id={"blk": to_blk, "win": to_win},
            device_id_type=pl.DeviceIdType.MESH,
        )

    bits = []
    bit = n_win // 2
    while bit:
        bits.append(bit)
        bit //= 2

    def direct(step):
        dest = (blk + step) % n_blk
        return remote(
            pair_ref.at[:, :, dest], got_ref.at[:, win, :, blk],
            pair_send.at[step], pair_recv.at[step], dest, win,
        )

    user = blk // per_share
    place = blk % per_share

    def own(step):
        dest = (blk + step) % n_blk
        return remote(
            own_ref.at[:, dest], src_ref.at[win, :, place],
            own_send.at[step], own_recv.at[place * n_win + win], dest, user,
        )

    def passed(step, offset, over):
        origin = (blk + n_blk - step) % n_blk
        slot = win
        for each in bits:
            if offset & each:
                slot = flip(slot, each)
        target = got_ref.at[:, slot, :, origin]
        source = pair_ref.at[:, :, blk] if step == 0 and offset == 0 else target
        mark = (offset | over) - 1
        return remote(
            source, target, pass_send.at[mark, step], pass_recv.at[mark, step], blk, flip(win, over)
        )

    rows = pair_ref.shape[1]
    half = rows // 2
    keep = pltpu.make_async_copy(
        pair_ref.at[:, :, blk], got_ref.at[:, win, :, blk], local_sem.at[0]
    )
    keep.start()
    is_user = user == win

    def own_keep():
        return pltpu.make_async_copy(
            own_ref.at[:, blk], src_ref.at[win, :, place], local_sem.at[1]
        )

    @pl.when(is_user)
    def _():
        own_keep().start()

    passes = []
    held = [0]
    for over in bits:
        passes.extend((offset, over) for offset in held)
        held = held + [offset | over for offset in held]

    sends = []
    for offset, over in passes:
        if offset == 0:
            copy = passed(0, 0, over)
            copy.start()
            sends.append(copy)
    for step in range(1, n_blk):
        copy = direct(step)
        copy.start()
        sends.append(copy)
    for step in range(1, n_blk):
        copy = own(step)
        copy.start()
        sends.append(copy)

    @pl.when(jnp.logical_not(is_user))
    def _():
        own(0).start()

    keep.wait()

    @pl.when(is_user)
    def _():
        own_keep().wait()

    waited = set()

    def arrive(step, offset):
        if (step, offset) in waited:
            return
        waited.add((step, offset))
        if offset == 0:
            if step:
                direct(step).wait_recv()
        else:
            over = offset & -offset
            passed(step, offset - over, over).wait_recv()

    def finish(step):
        for offset in held:
            arrive(step, offset)
        origin = (blk + n_blk - step) % n_blk

        for index in range(rounds):

            def store(peer, white):
                right_refs[index][pl.ds(peer * rows, rows), origin] = white

            whiten_into(lambda peer: got_ref[index, peer, :, origin], store, n_win, rows)

    for step in range(n_blk + 1):
        if 1 <= step < n_blk:
            arrive(step, 0)
            for offset, over in passes:
                if offset == 0:
                    copy = passed(step, 0, over)
                    copy.start()
                    sends.append(copy)
        if step >= 1:
            for offset, over in passes:
                if offset:
                    arrive(step - 1, offset)
                    copy = passed(step - 1, offset, over)
                    copy.start()
                    sends.append(copy)
        if step >= 2:
            finish(step - 2)
    finish(n_blk - 1)
    for local in range(per_share):
        for peer in range(n_win):
            here = jnp.logical_and(blk == win * per_share + local, win == peer)

            @pl.when(jnp.logical_not(here))
            def _():
                piece = src_ref.at[peer, :, local]
                remote(
                    piece, piece, own_send.at[0], own_recv.at[local * n_win + peer], blk, win
                ).wait_recv()

    def one_shard(local, carry):
        def store(peer, white):
            both_ref[0, pl.ds(peer * rows, rows), local] = white
            both_ref[1, pl.ds(peer * rows, half), local] = white[half:]
            both_ref[1, pl.ds(peer * rows + half, half), local] = -white[:half]

        whiten_into(lambda peer: src_ref[peer, :, local], store, n_win, rows)
        return carry

    lax.fori_loop(0, per_share, one_shard, 0)

    for copy in sends:
        copy.wait_send()

    @pl.when(jnp.logical_not(is_user))
    def _():
        own(0).wait_send()


def exchange(pair, own, n_blk, n_win):
    rounds, rows, _, per_peer, nbins = pair.shape
    per_share = n_blk // n_win
    dtype = pair.dtype
    anywhere = pl.BlockSpec(memory_space=pl.ANY)
    vmem = pl.BlockSpec(memory_space=pltpu.VMEM)
    depth = n_win * rows
    return pl.pallas_call(
        functools.partial(exchange_kernel, n_blk, n_win, rounds),
        out_shape=(
            *[jax.ShapeDtypeStruct((depth, n_blk, per_peer, nbins), dtype)] * rounds,
            jax.ShapeDtypeStruct((2, depth, per_share, per_peer, nbins), dtype),
        ),
        in_specs=[anywhere, anywhere],
        out_specs=(vmem,) * (rounds + 1),
        scratch_shapes=[
            pltpu.VMEM((rounds, n_win, rows, n_blk, per_peer, nbins), dtype),
            pltpu.VMEM((n_win, rows, per_share, per_peer, nbins), dtype),
            pltpu.SemaphoreType.DMA((n_blk,)),
            pltpu.SemaphoreType.DMA((n_blk,)),
            pltpu.SemaphoreType.DMA((n_win - 1, n_blk)),
            pltpu.SemaphoreType.DMA((n_win - 1, n_blk)),
            pltpu.SemaphoreType.DMA((n_blk,)),
            pltpu.SemaphoreType.DMA((n_blk,)),
            pltpu.SemaphoreType.DMA((2,)),
        ],
        compiler_params=pltpu.CompilerParams(collective_id=0, has_side_effects=True),
    )(pair, own)


def body(spectra, channel_slot, partners):
    n_blk = lax.axis_size("blk")
    n_win = lax.axis_size("win")
    parts, mine, chans, nbins = spectra.shape
    rows = parts * mine
    per_peer = chans // n_blk
    here = lax.axis_index("blk")
    share = chans // n_win
    windows = mine * n_win
    flat = spectra.reshape(rows, chans, nbins)
    wanted = jnp.concatenate([partners, jnp.arange(n_blk, dtype=jnp.int32)[None]], axis=0)
    slots = (
        wanted[:, :, None] * chans
        + here * per_peer
        + jnp.arange(per_peer, dtype=jnp.int32)[None, None, :]
    )
    selector = (slots[..., None] == channel_slot).astype(jnp.bfloat16)
    pair = jnp.einsum(
        "tzqc,xcf->txzqf", selector[:ROUNDS], flat, preferred_element_type=jnp.float32
    ).astype(jnp.bfloat16)
    own = jnp.einsum(
        "zqc,xcf->xzqf", selector[ROUNDS], flat, preferred_element_type=jnp.float32
    ).astype(jnp.bfloat16)
    *right, both = exchange(pair, own, n_blk, n_win)
    right = [each.reshape(n_win * rows, chans, nbins) for each in right]
    both = both.reshape(2, n_win * rows, share, nbins)
    table = lag_table(nbins, L, windows).reshape(2, nbins, L).astype(jnp.bfloat16)
    results = [correlate(both, right[index], table) for index in range(ROUNDS)]
    return jnp.stack(results, axis=0).transpose(0, 2, 1, 3)


def solution(mesh):
    in_specs = (P(None, "win", ("groups", "blk"), None), P(("groups", "blk")), P())
    out_specs = P(None, ("groups", "blk", "win"), None, None)
    return jax.shard_map(body, mesh=mesh, in_specs=in_specs, out_specs=out_specs, check_vma=False)
```

```python
import functools
import math

import jax
import jax.numpy as jnp
from jax import lax
from jax.experimental import pallas as pl
from jax.experimental.pallas import tpu as pltpu
from jax.sharding import PartitionSpec as P

L = 101
ROUNDS = 2


eps_power = 1e-06
half_band = 2
tile_rows = 8


def whiten_into(piece, store, n_win, rows):
    power = None
    for win in range(n_win):
        value_array = piece(win).astype(jnp.float32)
        part = jnp.sum(value_array * value_array, axis=0)
        power = part if power is None else power + part
    nbins = power.shape[1]
    padding = jnp.zeros((power.shape[0], half_band), jnp.float32)
    padded = jnp.concatenate([padding, power, padding], axis=1)
    total = padded[:, 0:nbins]
    for offset in range(1, 2 * half_band + 1):
        total = total + padded[:, offset : offset + nbins]
    place = lax.broadcasted_iota(jnp.int32, power.shape, 1)
    count = 1 + jnp.minimum(place, half_band) + jnp.minimum(nbins - 1 - place, half_band)
    level = total / (count.astype(jnp.float32) * (n_win * rows // 2))
    scale = lax.rsqrt(level + eps_power)
    for win in range(n_win):
        store(win, (piece(win).astype(jnp.float32) * scale).astype(jnp.bfloat16))


def lag_table(nbins, nlags, windows):
    samples = 2 * (nbins - 1)
    freq = jnp.arange(nbins, dtype=jnp.int32)
    lags = jnp.arange(nlags, dtype=jnp.int32) - (nlags - 1) // 2
    phase_index = freq[:, None] * lags[None, :] % samples
    angle = 2.0 * math.pi / samples * phase_index.astype(jnp.float32)
    weight = jnp.where((freq == 0) | (freq == nbins - 1), 1.0, 2.0).astype(jnp.float32)
    norm = 1.0 / math.sqrt(windows * samples)
    cos_part = weight[:, None] * jnp.cos(angle) * norm
    sin_part = -weight[:, None] * jnp.sin(angle) * norm
    return jnp.concatenate([cos_part, sin_part], axis=0)


def correlate(both, right, table):
    cross = jnp.einsum(
        "cwak,wbk->kcab", both, right, preferred_element_type=jnp.float32
    ).astype(jnp.bfloat16)
    return jnp.einsum(
        "kcab,ckl->lab", cross, table, preferred_element_type=jnp.float32
    ).astype(jnp.bfloat16)


def flip(index, bit):
    return index + bit - 2 * bit * ((index // bit) % 2)


def exchange_kernel(
    n_blk, n_win, rounds, pair_ref, own_ref, *refs
):
    right_refs = refs[:rounds]
    both_ref, got_ref, src_ref, pair_send, pair_recv = refs[rounds : rounds + 5]
    pass_send, pass_recv, own_send, own_recv, local_sem = refs[rounds + 5 :]
    blk = lax.axis_index("blk")
    win = lax.axis_index("win")
    per_share = n_blk // n_win
    barrier = pltpu.get_barrier_semaphore()
    for step in range(1, n_blk * n_win):
        other = (blk * n_win + win + step) % (n_blk * n_win)
        pl.semaphore_signal(
            barrier,
            inc=1,
            device_id={"blk": other // n_win, "win": other % n_win},
            device_id_type=pl.DeviceIdType.MESH,
        )
    pl.semaphore_wait(barrier, n_blk * n_win - 1)

    def remote(src, dst, send, recv, to_blk, to_win):
        return pltpu.make_async_remote_copy(
            src_ref=src,
            dst_ref=dst,
            send_sem=send,
            recv_sem=recv,
            device_id={"blk": to_blk, "win": to_win},
            device_id_type=pl.DeviceIdType.MESH,
        )

    bits = []
    bit = n_win // 2
    while bit:
        bits.append(bit)
        bit //= 2

    order = [0] + list(range(n_blk - 1, 0, -1))

    def across(step):
        other, each = blk, 1
        while each < n_blk:
            if step & each:
                other = flip(other, each)
            each *= 2
        return other

    def direct(step):
        dest = across(step)
        return remote(
            pair_ref.at[:, :, dest], got_ref.at[:, win, :, blk],
            pair_send.at[step], pair_recv.at[step], dest, win,
        )

    user = blk // per_share
    place = blk % per_share

    def own(step):
        dest = across(step)
        return remote(
            own_ref.at[:, dest], src_ref.at[win, :, place],
            own_send.at[step], own_recv.at[place * n_win + win], dest, user,
        )

    def passed(step, offset, over):
        origin = across(step)
        slot = win
        for each in bits:
            if offset & each:
                slot = flip(slot, each)
        target = got_ref.at[:, slot, :, origin]
        source = pair_ref.at[:, :, blk] if step == 0 and offset == 0 else target
        mark = (offset | over) - 1
        return remote(
            source, target, pass_send.at[mark, step], pass_recv.at[mark, step], blk, flip(win, over)
        )

    rows = pair_ref.shape[1]
    half = rows // 2
    keep = pltpu.make_async_copy(
        pair_ref.at[:, :, blk], got_ref.at[:, win, :, blk], local_sem.at[0]
    )
    keep.start()
    is_user = user == win

    def own_keep():
        return pltpu.make_async_copy(
            own_ref.at[:, blk], src_ref.at[win, :, place], local_sem.at[1]
        )

    @pl.when(is_user)
    def _():
        own_keep().start()

    passes = []
    held = [0]
    for over in bits:
        passes.extend((offset, over) for offset in held)
        held = held + [offset | over for offset in held]

    sends = []
    for offset, over in passes:
        if offset == 0:
            copy = passed(0, 0, over)
            copy.start()
            sends.append(copy)
    for step in order[1:]:
        copy = direct(step)
        copy.start()
        sends.append(copy)
    for step in order[1:]:
        copy = own(step)
        copy.start()
        sends.append(copy)

    @pl.when(jnp.logical_not(is_user))
    def _():
        own(0).start()

    keep.wait()

    @pl.when(is_user)
    def _():
        own_keep().wait()

    waited = set()

    def arrive(step, offset):
        if (step, offset) in waited:
            return
        waited.add((step, offset))
        if offset == 0:
            if step:
                direct(step).wait_recv()
        else:
            over = offset & -offset
            passed(step, offset - over, over).wait_recv()

    def finish(step):
        for offset in held:
            arrive(step, offset)
        origin = across(step)

        for index in range(rounds):

            def store(peer, white):
                right_refs[index][pl.ds(peer * rows, rows), origin] = white

            whiten_into(lambda peer: got_ref[index, peer, :, origin], store, n_win, rows)

    for turn in range(n_blk + 1):
        if 1 <= turn < n_blk:
            step = order[turn]
            arrive(step, 0)
            for offset, over in passes:
                if offset == 0:
                    copy = passed(step, 0, over)
                    copy.start()
                    sends.append(copy)
        if turn >= 1:
            step = order[turn - 1]
            for offset, over in passes:
                if offset:
                    arrive(step, offset)
                    copy = passed(step, offset, over)
                    copy.start()
                    sends.append(copy)
        if turn >= 2:
            finish(order[turn - 2])
    finish(order[n_blk - 1])
    for local in range(per_share):
        for peer in range(n_win):
            here = jnp.logical_and(blk == win * per_share + local, win == peer)

            @pl.when(jnp.logical_not(here))
            def _():
                piece = src_ref.at[peer, :, local]
                remote(
                    piece, piece, own_send.at[0], own_recv.at[local * n_win + peer], blk, win
                ).wait_recv()

    def one_shard(local, carry):
        def store(peer, white):
            both_ref[0, pl.ds(peer * rows, rows), local] = white
            both_ref[1, pl.ds(peer * rows, half), local] = white[half:]
            both_ref[1, pl.ds(peer * rows + half, half), local] = -white[:half]

        whiten_into(lambda peer: src_ref[peer, :, local], store, n_win, rows)
        return carry

    lax.fori_loop(0, per_share, one_shard, 0)

    for copy in sends:
        copy.wait_send()

    @pl.when(jnp.logical_not(is_user))
    def _():
        own(0).wait_send()


def exchange(pair, own, n_blk, n_win):
    rounds, rows, _, per_peer, nbins = pair.shape
    per_share = n_blk // n_win
    dtype = pair.dtype
    anywhere = pl.BlockSpec(memory_space=pl.ANY)
    vmem = pl.BlockSpec(memory_space=pltpu.VMEM)
    depth = n_win * rows
    return pl.pallas_call(
        functools.partial(exchange_kernel, n_blk, n_win, rounds),
        out_shape=(
            *[jax.ShapeDtypeStruct((depth, n_blk, per_peer, nbins), dtype)] * rounds,
            jax.ShapeDtypeStruct((2, depth, per_share, per_peer, nbins), dtype),
        ),
        in_specs=[anywhere, anywhere],
        out_specs=(vmem,) * (rounds + 1),
        scratch_shapes=[
            pltpu.VMEM((rounds, n_win, rows, n_blk, per_peer, nbins), dtype),
            pltpu.VMEM((n_win, rows, per_share, per_peer, nbins), dtype),
            pltpu.SemaphoreType.DMA((n_blk,)),
            pltpu.SemaphoreType.DMA((n_blk,)),
            pltpu.SemaphoreType.DMA((n_win - 1, n_blk)),
            pltpu.SemaphoreType.DMA((n_win - 1, n_blk)),
            pltpu.SemaphoreType.DMA((n_blk,)),
            pltpu.SemaphoreType.DMA((n_blk,)),
            pltpu.SemaphoreType.DMA((2,)),
        ],
        compiler_params=pltpu.CompilerParams(collective_id=0, has_side_effects=True),
    )(pair, own)


def body(spectra, channel_slot, partners):
    n_blk = lax.axis_size("blk")
    n_win = lax.axis_size("win")
    parts, mine, chans, nbins = spectra.shape
    rows = parts * mine
    per_peer = chans // n_blk
    here = lax.axis_index("blk")
    share = chans // n_win
    windows = mine * n_win
    flat = spectra.reshape(rows, chans, nbins)
    wanted = jnp.concatenate([partners, jnp.arange(n_blk, dtype=jnp.int32)[None]], axis=0)
    slots = (
        wanted[:, :, None] * chans
        + here * per_peer
        + jnp.arange(per_peer, dtype=jnp.int32)[None, None, :]
    )
    selector = (slots[..., None] == channel_slot).astype(jnp.bfloat16)
    pair = jnp.einsum(
        "tzqc,xcf->txzqf", selector[:ROUNDS], flat, preferred_element_type=jnp.float32
    ).astype(jnp.bfloat16)
    own = jnp.einsum(
        "zqc,xcf->xzqf", selector[ROUNDS], flat, preferred_element_type=jnp.float32
    ).astype(jnp.bfloat16)
    *right, both = exchange(pair, own, n_blk, n_win)
    right = [each.reshape(n_win * rows, chans, nbins) for each in right]
    both = both.reshape(2, n_win * rows, share, nbins)
    table = lag_table(nbins, L, windows).reshape(2, nbins, L).astype(jnp.bfloat16)
    results = [correlate(both, right[index], table) for index in range(ROUNDS)]
    return jnp.stack(results, axis=0).transpose(0, 2, 1, 3)


def solution(mesh):
    in_specs = (P(None, "win", ("groups", "blk"), None), P(("groups", "blk")), P())
    out_specs = P(None, ("groups", "blk", "win"), None, None)
    return jax.shard_map(body, mesh=mesh, in_specs=in_specs, out_specs=out_specs, check_vma=False)
```

```python
import functools
import math

import jax
import jax.numpy as jnp
from jax import lax
from jax.experimental import pallas as pl
from jax.experimental.pallas import tpu as pltpu
from jax.sharding import PartitionSpec as P

L = 101
ROUNDS = 2


eps_power = 1e-06
half_band = 2
tile_rows = 8


def whiten_into(piece, store, n_win, rows):
    power = None
    for win in range(n_win):
        value_array = piece(win).astype(jnp.float32)
        part = jnp.sum(value_array * value_array, axis=0)
        power = part if power is None else power + part
    nbins = power.shape[1]
    padding = jnp.zeros((power.shape[0], half_band), jnp.float32)
    padded = jnp.concatenate([padding, power, padding], axis=1)
    total = padded[:, 0:nbins]
    for offset in range(1, 2 * half_band + 1):
        total = total + padded[:, offset : offset + nbins]
    place = lax.broadcasted_iota(jnp.int32, power.shape, 1)
    count = 1 + jnp.minimum(place, half_band) + jnp.minimum(nbins - 1 - place, half_band)
    level = total / (count.astype(jnp.float32) * (n_win * rows // 2))
    scale = lax.rsqrt(level + eps_power)
    for win in range(n_win):
        store(win, (piece(win).astype(jnp.float32) * scale).astype(jnp.bfloat16))


def lag_table(nbins, nlags, windows):
    samples = 2 * (nbins - 1)
    freq = jnp.arange(nbins, dtype=jnp.int32)
    lags = jnp.arange(nlags, dtype=jnp.int32) - (nlags - 1) // 2
    phase_index = freq[:, None] * lags[None, :] % samples
    angle = 2.0 * math.pi / samples * phase_index.astype(jnp.float32)
    weight = jnp.where((freq == 0) | (freq == nbins - 1), 1.0, 2.0).astype(jnp.float32)
    norm = 1.0 / math.sqrt(windows * samples)
    cos_part = weight[:, None] * jnp.cos(angle) * norm
    sin_part = -weight[:, None] * jnp.sin(angle) * norm
    return jnp.concatenate([cos_part, sin_part], axis=0)


def correlate(both, right, table):
    cross = jnp.einsum(
        "cwak,wbk->kcab", both, right, preferred_element_type=jnp.float32
    ).astype(jnp.bfloat16)
    return jnp.einsum(
        "kcab,ckl->lab", cross, table, preferred_element_type=jnp.float32
    ).astype(jnp.bfloat16)


def flip(index, bit):
    return index + bit - 2 * bit * ((index // bit) % 2)


def exchange_kernel(
    n_blk, n_win, rounds, pair_ref, own_ref, *refs
):
    right_refs = refs[:rounds]
    both_ref, got_ref, src_ref, pair_send, pair_recv = refs[rounds : rounds + 5]
    pass_send, pass_recv, own_send, own_recv, local_sem = refs[rounds + 5 :]
    blk = lax.axis_index("blk")
    win = lax.axis_index("win")
    per_share = n_blk // n_win
    barrier = pltpu.get_barrier_semaphore()
    for step in range(1, n_blk * n_win):
        other = (blk * n_win + win + step) % (n_blk * n_win)
        pl.semaphore_signal(
            barrier,
            inc=1,
            device_id={"blk": other // n_win, "win": other % n_win},
            device_id_type=pl.DeviceIdType.MESH,
        )
    pl.semaphore_wait(barrier, n_blk * n_win - 1)

    def remote(src, dst, send, recv, to_blk, to_win):
        return pltpu.make_async_remote_copy(
            src_ref=src,
            dst_ref=dst,
            send_sem=send,
            recv_sem=recv,
            device_id={"blk": to_blk, "win": to_win},
            device_id_type=pl.DeviceIdType.MESH,
        )

    bits = []
    bit = n_win // 2
    while bit:
        bits.append(bit)
        bit //= 2

    order = list(range(n_blk))

    def across(step):
        other, each = blk, 1
        while each < n_blk:
            if step & each:
                other = flip(other, each)
            each *= 2
        return other

    def direct(step):
        dest = across(step)
        return remote(
            pair_ref.at[:, :, dest], got_ref.at[:, win, :, blk],
            pair_send.at[step], pair_recv.at[step], dest, win,
        )

    user = blk // per_share
    place = blk % per_share

    def own(step):
        dest = across(step)
        return remote(
            own_ref.at[:, dest], src_ref.at[win, :, place],
            own_send.at[step], own_recv.at[place * n_win + win], dest, user,
        )

    def passed(step, offset, over):
        origin = across(step)
        slot = win
        for each in bits:
            if offset & each:
                slot = flip(slot, each)
        target = got_ref.at[:, slot, :, origin]
        source = pair_ref.at[:, :, blk] if step == 0 and offset == 0 else target
        mark = (offset | over) - 1
        return remote(
            source, target, pass_send.at[mark, step], pass_recv.at[mark, step], blk, flip(win, over)
        )

    rows = pair_ref.shape[1]
    half = rows // 2
    keep = pltpu.make_async_copy(
        pair_ref.at[:, :, blk], got_ref.at[:, win, :, blk], local_sem.at[0]
    )
    keep.start()
    is_user = user == win

    def own_keep():
        return pltpu.make_async_copy(
            own_ref.at[:, blk], src_ref.at[win, :, place], local_sem.at[1]
        )

    @pl.when(is_user)
    def _():
        own_keep().start()

    passes = []
    held = [0]
    for over in bits:
        passes.extend((offset, over) for offset in held)
        held = held + [offset | over for offset in held]

    sends = []
    for offset, over in passes:
        if offset == 0:
            copy = passed(0, 0, over)
            copy.start()
            sends.append(copy)
    for step in order[1:]:
        copy = direct(step)
        copy.start()
        sends.append(copy)
    for step in order[1:]:
        copy = own(step)
        copy.start()
        sends.append(copy)

    @pl.when(jnp.logical_not(is_user))
    def _():
        own(0).start()

    keep.wait()

    @pl.when(is_user)
    def _():
        own_keep().wait()

    waited = set()

    def arrive(step, offset):
        if (step, offset) in waited:
            return
        waited.add((step, offset))
        if offset == 0:
            if step:
                direct(step).wait_recv()
        else:
            over = offset & -offset
            passed(step, offset - over, over).wait_recv()

    def finish(step):
        for offset in held:
            arrive(step, offset)
        origin = across(step)

        for index in range(rounds):

            def store(peer, white):
                right_refs[index][pl.ds(peer * rows, rows), origin] = white

            whiten_into(lambda peer: got_ref[index, peer, :, origin], store, n_win, rows)

    for turn in range(n_blk + 1):
        if 1 <= turn < n_blk:
            step = order[turn]
            arrive(step, 0)
            for offset, over in passes:
                if offset == 0:
                    copy = passed(step, 0, over)
                    copy.start()
                    sends.append(copy)
        if turn >= 1:
            step = order[turn - 1]
            for offset, over in passes:
                if offset:
                    arrive(step, offset)
                    copy = passed(step, offset, over)
                    copy.start()
                    sends.append(copy)
        if turn >= 2:
            finish(order[turn - 2])
    finish(order[n_blk - 1])
    for local in range(per_share):
        for peer in range(n_win):
            here = jnp.logical_and(blk == win * per_share + local, win == peer)

            @pl.when(jnp.logical_not(here))
            def _():
                piece = src_ref.at[peer, :, local]
                remote(
                    piece, piece, own_send.at[0], own_recv.at[local * n_win + peer], blk, win
                ).wait_recv()

    def one_shard(local, carry):
        def store(peer, white):
            both_ref[0, pl.ds(peer * rows, rows), local] = white
            both_ref[1, pl.ds(peer * rows, half), local] = white[half:]
            both_ref[1, pl.ds(peer * rows + half, half), local] = -white[:half]

        whiten_into(lambda peer: src_ref[peer, :, local], store, n_win, rows)
        return carry

    lax.fori_loop(0, per_share, one_shard, 0)

    for copy in sends:
        copy.wait_send()

    @pl.when(jnp.logical_not(is_user))
    def _():
        own(0).wait_send()


def exchange(pair, own, n_blk, n_win):
    rounds, rows, _, per_peer, nbins = pair.shape
    per_share = n_blk // n_win
    dtype = pair.dtype
    anywhere = pl.BlockSpec(memory_space=pl.ANY)
    vmem = pl.BlockSpec(memory_space=pltpu.VMEM)
    depth = n_win * rows
    return pl.pallas_call(
        functools.partial(exchange_kernel, n_blk, n_win, rounds),
        out_shape=(
            *[jax.ShapeDtypeStruct((depth, n_blk, per_peer, nbins), dtype)] * rounds,
            jax.ShapeDtypeStruct((2, depth, per_share, per_peer, nbins), dtype),
        ),
        in_specs=[anywhere, anywhere],
        out_specs=(vmem,) * (rounds + 1),
        scratch_shapes=[
            pltpu.VMEM((rounds, n_win, rows, n_blk, per_peer, nbins), dtype),
            pltpu.VMEM((n_win, rows, per_share, per_peer, nbins), dtype),
            pltpu.SemaphoreType.DMA((n_blk,)),
            pltpu.SemaphoreType.DMA((n_blk,)),
            pltpu.SemaphoreType.DMA((n_win - 1, n_blk)),
            pltpu.SemaphoreType.DMA((n_win - 1, n_blk)),
            pltpu.SemaphoreType.DMA((n_blk,)),
            pltpu.SemaphoreType.DMA((n_blk,)),
            pltpu.SemaphoreType.DMA((2,)),
        ],
        compiler_params=pltpu.CompilerParams(collective_id=0, has_side_effects=True),
    )(pair, own)


def body(spectra, channel_slot, partners):
    n_blk = lax.axis_size("blk")
    n_win = lax.axis_size("win")
    parts, mine, chans, nbins = spectra.shape
    rows = parts * mine
    per_peer = chans // n_blk
    here = lax.axis_index("blk")
    share = chans // n_win
    windows = mine * n_win
    flat = spectra.reshape(rows, chans, nbins)
    wanted = jnp.concatenate([partners, jnp.arange(n_blk, dtype=jnp.int32)[None]], axis=0)
    slots = (
        wanted[:, :, None] * chans
        + here * per_peer
        + jnp.arange(per_peer, dtype=jnp.int32)[None, None, :]
    )
    selector = (slots[..., None] == channel_slot).astype(jnp.bfloat16)
    pair = jnp.einsum(
        "tzqc,xcf->txzqf", selector[:ROUNDS], flat, preferred_element_type=jnp.float32
    ).astype(jnp.bfloat16)
    own = jnp.einsum(
        "zqc,xcf->xzqf", selector[ROUNDS], flat, preferred_element_type=jnp.float32
    ).astype(jnp.bfloat16)
    *right, both = exchange(pair, own, n_blk, n_win)
    right = [each.reshape(n_win * rows, chans, nbins) for each in right]
    both = both.reshape(2, n_win * rows, share, nbins)
    table = lag_table(nbins, L, windows).reshape(2, nbins, L).astype(jnp.bfloat16)
    results = [correlate(both, right[index], table) for index in range(ROUNDS)]
    return jnp.stack(results, axis=0).transpose(0, 2, 1, 3)


def solution(mesh):
    in_specs = (P(None, "win", ("groups", "blk"), None), P(("groups", "blk")), P())
    out_specs = P(None, ("groups", "blk", "win"), None, None)
    return jax.shard_map(body, mesh=mesh, in_specs=in_specs, out_specs=out_specs, check_vma=False)
```
